32 devices in a mesh: row: 4 (over y, x), col: 4 (over z), layer: 2 (over core).
Axes of the slice: x: 2, y: 2, z: 4, core: 2. Of those that a mesh axis runs over, the one named last changes fastest.
Arguments:
- panel_rows: bfloat16 [12, 8, 2048, 256], P('layer', 'row', 'col'), may hold values from -0.625 to 0.625
- panel_cols: bfloat16 [12, 16, 2048, 256], P('layer', 'col', 'row'), may hold values from -0.625 to 0.625
- rank_rows: int32 [12, 8], P('layer', 'row'), may hold values from 32 to 128, as said below
- rank_cols: int32 [12, 16], P('layer', 'col'), may hold values from 32 to 128, as said below
- trailing: bfloat16 [8, 16, 2048, 128], P('row', 'col'), may hold values from -1.75 to 1.75
- sketch: bfloat16 [2048, 64], replicated, may hold values from -6 to 6
Outputs:
- new_basis: bfloat16 [8, 16, 2048, 64], P('row', 'col', 'layer')
- new_core: bfloat16 [8, 16, 2048, 64], P('row', 'col', 'layer')
The draws below stay inside these ranges and needn't reach their ends.
Inputs may be any that keep to these rules, and one draw needn't show every extreme that they name: `rank_rows`: rank of each panel tile of the rows; every draw holds both ends. `rank_cols`: rank of each panel tile of the columns; every draw holds both ends.
All inputs are finite; a program needn't handle non-finite values.
Results may differ from the reference program's by a relative error of at most 0.014.
Values may be sent and summed in bfloat16 or wider, within the bound.
No kernel may reach another device: no remote copies, remote signals or barrier semaphores. Data moves between devices by JAX's collectives and lax.ppermute only.
A program may use at most 128 MiB of HBM per device.

```python
import math
import jax
import jax.numpy as jnp
from jax import lax

B = 2048
RANK = 128
RC = 64
PANEL_DEV = 6
PANELS = 12
NI = 8
NJ = 16


def rank_table(key, count):
    first, second, third = jax.random.split(key, 3)
    total = PANELS * count
    values = jax.random.randint(first, (total,), RANK // 4, RANK + 1)
    high_spot = jax.random.randint(second, (), 0, total)
    low_spot = (high_spot + 1 + jax.random.randint(third, (), 0, total - 1)) % total
    spots = jnp.arange(total)
    values = jnp.where(spots == high_spot, RANK, values)
    values = jnp.where(spots == low_spot, RANK // 4, values)
    return values.reshape(PANELS, count).astype(jnp.int32)


def draw_rank_rows(key, part):
    return rank_table(jax.random.fold_in(key, 101), NI)


def draw_rank_cols(key, part):
    return rank_table(jax.random.fold_in(key, 202), NJ)


def block_scale(key, shape, cuts, low, top_value):
    level = 1.0
    for position, blocks in cuts:
        steps = jax.random.uniform(jax.random.fold_in(jax.random.fold_in(key, 6), position), (blocks,), jnp.float32, low / len(cuts), top_value / len(cuts))
        level = level * jnp.repeat(jnp.exp(steps), shape[position] // blocks).reshape((-1,) + (1,) * (len(shape) - 1 - position))
    return level


def normal_values(stream_key, extent, scale, bound, pieces=(), kind=jnp.bfloat16):
    level = block_scale(stream_key, extent, pieces, -0.22, 0.18) if pieces else 1.0
    result = jax.random.normal(stream_key, extent, jnp.float32) * scale * level
    return jnp.minimum(jnp.maximum(result, -bound), bound).astype(kind)


def setup_inputs(seed: int = 0) -> dict:
    key_list = jax.random.split(jax.random.key(seed), 7)
    return {
        "panel_rows": normal_values(key_list[0], (PANELS, NI, B, 2 * RANK), (RANK * 3 // 5) ** -0.5, 0.625, ((0, 2), (1, 4), (2, 4))),
        "panel_cols": normal_values(key_list[1], (PANELS, NJ, B, 2 * RANK), (RANK * 3 // 5) ** -0.5, 0.625, ((0, 2), (1, 4), (2, 4))),
        "rank_rows": draw_rank_rows(jax.random.fold_in(key_list[6], 71), 0),
        "rank_cols": draw_rank_cols(jax.random.fold_in(key_list[6], 71), 0),
        "trailing": normal_values(key_list[4], (NI, NJ, B, 2 * RC), (RC // 8 + 4) ** -0.5, 1.75, ((0, 4), (1, 4))),
        "sketch": normal_values(key_list[5], (B, RC), 1.0, 6.0),
    }


def keep_ranks(panel, ranks):
    width = panel.shape[-1] // 2
    kept = (jnp.arange(width)[None, None, :] < ranks[:, :, None]).astype(panel.dtype)
    return panel * jnp.concatenate([kept, kept], axis=-1)[:, :, None, :]

def rounded(value):
    return lax.optimization_barrier(value.astype(jnp.bfloat16)).astype(jnp.float32)

def reference(panel_rows, panel_cols, rank_rows, rank_cols, trailing, sketch):
    groups = PANELS // PANEL_DEV
    rows_masked = keep_ranks(panel_rows, rank_rows)
    cols_masked = keep_ranks(panel_cols, rank_cols)
    col_left = cols_masked[..., :RANK].astype(jnp.float32)
    col_right = cols_masked[..., RANK:].astype(jnp.float32)
    sketch_wide = sketch.astype(jnp.float32)
    probe = rounded(jnp.einsum('kjbr,bc->kjrc', col_left, sketch_wide))
    col_grouped = col_left.reshape(groups, PANEL_DEV, NJ, B, RANK)

    def one_row(packed):
        row_tile, tile_row = packed
        row_left = row_tile[..., :RANK].astype(jnp.float32)
        row_right = row_tile[..., RANK:].astype(jnp.float32)
        inner = rounded(jnp.einsum('kbr,kjbs->kjrs', row_right, col_right))
        mixed = rounded(jnp.einsum('kjrs,kjsc->kjrc', inner, probe))
        row_grouped = row_left.reshape(groups, PANEL_DEV, B, RANK)
        parts = jnp.einsum('lpbr,lpjrc->ljbc', row_grouped, mixed.reshape(groups, PANEL_DEV, NJ, RANK, RC))
        panel_sketch = lax.optimization_barrier(jnp.sum(rounded(parts), axis=0))
        tile_left = tile_row[..., :RC].astype(jnp.float32)
        tile_right = tile_row[..., RC:].astype(jnp.float32)
        tile_probe = rounded(jnp.einsum('jbc,bd->jcd', tile_right, sketch_wide))
        sampled = jnp.einsum('jbc,jcd->jbd', tile_left, tile_probe) - panel_sketch
        gram_matrix = jnp.einsum('jbc,jbd->jcd', sampled, sampled, precision=lax.Precision.HIGHEST) / B
        factor = jnp.linalg.cholesky(gram_matrix)
        basis_full = lax.linalg.triangular_solve(factor, sampled, left_side=False, lower=True, transpose_a=True)
        basis_low = lax.optimization_barrier(basis_full.astype(jnp.bfloat16))
        basis_wide = basis_low.astype(jnp.float32)
        projected = rounded(jnp.einsum('kbr,jbc->kjrc', row_left, basis_wide))
        turned = rounded(jnp.einsum('kjrs,kjrc->kjsc', inner, projected))
        core_parts = jnp.einsum('lpjbs,lpjsc->ljbc', col_grouped, turned.reshape(groups, PANEL_DEV, NJ, RANK, RC))
        panel_core = lax.optimization_barrier(jnp.sum(rounded(core_parts), axis=0))
        tile_proj = rounded(jnp.einsum('jbc,jbd->jcd', tile_left, basis_wide))
        core_value = (jnp.einsum('jbc,jcd->jbd', tile_right, tile_proj) - panel_core) / math.sqrt(B)
        return (basis_low, core_value.astype(jnp.bfloat16))
    new_basis, new_core = lax.map(one_row, (jnp.swapaxes(rows_masked, 0, 1), trailing))
    return (new_basis, new_core)
```

```python
import functools
import math

import jax
import jax.numpy as jnp
from jax import lax
from jax.experimental import pallas as pl
from jax.experimental.pallas import tpu as pltpu
from jax.sharding import PartitionSpec as P

WIDE = jnp.float32
NARROW = jnp.bfloat16
ANY = pl.BlockSpec(memory_space=pl.ANY)
VMEM = pl.BlockSpec(memory_space=pltpu.VMEM)
SMEM = pl.BlockSpec(memory_space=pltpu.SMEM)


def product(a, b, dims, precision=None):
    return lax.dot_general(
        a, b, (dims, ((), ())), precision=precision, preferred_element_type=WIDE
    )


def rows_by_columns(a, b, precision=None):
    return product(a, b, ((1,), (0,)), precision)


def rows_by_rows(a, b, precision=None):
    return product(a, b, ((1,), (1,)), precision)


def cost(flops, moved):
    return pl.CostEstimate(flops=int(flops), bytes_accessed=int(moved), transcendentals=0)


def whole_gather(parts, axis):
    pieces = []
    for first, part in parts:
        full = lax.all_gather(part, axis)
        pieces += [(full[s], first, jnp.int32(s)) for s in range(full.shape[0])]
    return pieces


def line_gather(part, axis):
    if lax.axis_size(axis) != 4:
        return whole_gather([(0, part)], axis)
    place = lax.axis_index(axis)
    outer = (place == 0) | (place == 3)
    ends, middle, outward = [(0, 1), (1, 0), (2, 3), (3, 2)], [(1, 2), (2, 1)], [(1, 0), (2, 3)]
    near = lax.ppermute(part, axis, ends)
    across = lax.ppermute(part, axis, middle)
    across_far = lax.ppermute(near, axis, middle)
    passed = lax.ppermute(across, axis, outward)
    passed_far = lax.ppermute(across_far, axis, outward)
    return [
        (part, 0, place),
        (near, 0, place ^ 1),
        (across, 0, jnp.where(outer, -1, place ^ 3)),
        (across_far, 0, jnp.where(outer, -1, place ^ 2)),
        (passed, 0, jnp.where(outer, place ^ 2, -1)),
        (passed_far, 0, jnp.where(outer, place ^ 3, -1)),
    ]


def swap(part, axis, bit):
    return lax.ppermute(part, axis, [(n, n ^ bit) for n in range(lax.axis_size(axis))])


def square_gather(low, high, axis):
    half = low.shape[0]
    if lax.axis_size(axis) != 4:
        return whole_gather([(0, low), (half, high)], axis), None
    place = lax.axis_index(axis)
    low_x, low_y = swap(low, axis, 1), swap(low, axis, 2)
    high_x, high_y = swap(high, axis, 1), swap(high, axis, 2)
    low_far, high_far = swap(low_y, axis, 1), swap(high_x, axis, 2)
    pieces = [
        (low, 0, place),
        (high, half, place),
        (low_x, 0, place ^ 1),
        (high_x, half, place ^ 1),
        (low_y, 0, place ^ 2),
        (high_y, half, place ^ 2),
        (low_far, 0, place ^ 3),
        (high_far, half, place ^ 3),
    ]
    return pieces, (low_x, low_y)


def square_sum(low, high, axis):
    if lax.axis_size(axis) != 4:
        return lax.psum(low, axis), lax.psum(high, axis)
    low, high = low + swap(low, axis, 1), high + swap(high, axis, 2)
    return low + swap(low, axis, 2), high + swap(high, axis, 1)


def after(value, *earlier):
    earlier = [e for e in earlier if e is not None]
    return lax.optimization_barrier((value, *earlier))[0] if earlier else value


def each_piece(refs, firsts, slots, base, held, sems, act):
    for n, (ref, first) in enumerate(zip(refs, firsts)):
        slot = slots[base + n]

        @pl.when(slot >= 0)
        def _(ref=ref, first=first, slot=slot, n=n):
            rows = ref.shape[-2]
            lead = (pl.ds(first, ref.shape[0]),) + (slice(None),) * (len(ref.shape) - 3)
            start = pl.multiple_of(slot * rows, rows)
            target = held.at[lead + (pl.ds(start, rows), slice(None))]
            act(pltpu.make_async_copy(ref, target, sems.at[base + n]))


def unzip(pieces):
    arrays, firsts, slots = zip(*pieces)
    return list(arrays), list(firsts), [s.astype(jnp.int32) for s in slots]


def start(copy):
    copy.start()


def finish(copy):
    copy.wait()


def tile_body(sketch_ref, tile_ref, out_ref):
    tile = tile_ref[0, 0]
    both = rows_by_columns(sketch_ref[...], tile)
    turned = pltpu.roll(both, both.shape[1] // 2, 1)
    lane = lax.broadcasted_iota(jnp.int32, turned.shape, 1)
    probe = jnp.where(lane < turned.shape[1] // 2, turned, 0.0).astype(NARROW)
    out_ref[0] = rows_by_rows(probe, tile)


def tile_samples(sketch_t, trailing):
    ni, nj, order, both = trailing.shape
    c = sketch_t.shape[0]
    return pl.pallas_call(
        tile_body,
        grid=(ni, nj),
        in_specs=[
            pl.BlockSpec((c, order), lambda i, j: (0, 0)),
            pl.BlockSpec((1, 1, order, both), lambda i, j: (i, j, 0, 0)),
        ],
        out_specs=pl.BlockSpec((1, c, order), lambda i, j: (i, j, 0)),
        out_shape=jax.ShapeDtypeStruct((ni, nj * c, order), WIDE),
        cost_estimate=cost(4 * ni * nj * order * both * c, 4 * ni * nj * order * both),
        name="tile_samples",
    )(sketch_t, trailing)


def probe_body(place_ref, sketch_ref, left_ref, out_ref):
    for j in range(left_ref.shape[1]):
        out_ref[0, j] = rows_by_columns(sketch_ref[...], left_ref[0, j])


def probe_share(place, sketch_t, panel):
    k, nj, rows, both = panel.shape
    c = sketch_t.shape[0]
    width = both // 2
    return pl.pallas_call(
        probe_body,
        grid_spec=pltpu.PrefetchScalarGridSpec(
            num_scalar_prefetch=1,
            grid=(k,),
            in_specs=[
                pl.BlockSpec((c, rows), lambda n, place: (0, place[0])),
                pl.BlockSpec((1, nj, rows, width), lambda n, place: (n, 0, 0, 0)),
            ],
            out_specs=pl.BlockSpec((1, nj, c, width), lambda n, place: (n, 0, 0, 0)),
        ),
        out_shape=jax.ShapeDtypeStruct((k, nj, c, width), WIDE),
        cost_estimate=cost(2 * k * nj * rows * width * c, 2 * k * nj * rows * width),
        name="probe_share",
    )(place, sketch_t, panel)


def inner_body(
    row, row_firsts, col_firsts, slots, row_rank, col_rank, low_probe, high_probe, *refs
):
    nr, nc = len(row_firsts), len(col_firsts)
    row_refs, col_refs = refs[:nr], refs[nr : nr + nc]
    inner_ref, mixed_ref, row_held, col_held, sems = refs[nr + nc :]
    for act in (start, finish):
        each_piece(row_refs, row_firsts, slots, 0, row_held, sems, act)
        each_piece(col_refs, col_firsts, slots, nr, col_held, sems, act)
    panels, nj = col_held.shape[:2]
    width = col_held.shape[-1]
    half = low_probe.shape[0]

    def one(k, probe_ref, n):
        right = jnp.concatenate([col_held[k, j] for j in range(nj)], axis=1)
        value = product(row_held[k], right, ((0,), (0,)))
        r = lax.broadcasted_iota(jnp.int32, (width, width), 0)
        s = lax.broadcasted_iota(jnp.int32, (width, width), 1)
        mixed = []
        for j in range(nj):
            kept = (r < row_rank[k, row]) & (s < col_rank[k, j])
            block = jnp.where(kept, value[:, j * width : (j + 1) * width], 0.0).astype(NARROW)
            inner_ref[k, :, j * width : (j + 1) * width] = block
            mixed.append(rows_by_rows(probe_ref[n, j].astype(NARROW), block))
        mixed_ref[k] = jnp.concatenate(mixed, axis=0).astype(NARROW)

    @pl.loop(0, half)
    def _(n):
        one(n, low_probe, n)

    @pl.loop(0, panels - half)
    def _(n):
        one(n + half, high_probe, n)


def inner_and_mixed(row, rows, cols, row_rank, col_rank, low_probe, high_probe, order):
    row_arrays, row_firsts, row_slots = unzip(rows)
    col_arrays, col_firsts, col_slots = unzip(cols)
    slots = jnp.stack(row_slots + col_slots)
    panels, width = row_arrays[0].shape[0], row_arrays[0].shape[-1]
    nj = col_arrays[0].shape[1]
    c = low_probe.shape[2]
    return pl.pallas_call(
        functools.partial(inner_body, row, row_firsts, col_firsts),
        in_specs=[SMEM, SMEM, SMEM, VMEM, VMEM] + [ANY] * (len(rows) + len(cols)),
        out_specs=[VMEM, VMEM],
        out_shape=[
            jax.ShapeDtypeStruct((panels, width, nj * width), NARROW),
            jax.ShapeDtypeStruct((panels, nj * c, width), NARROW),
        ],
        scratch_shapes=[
            pltpu.VMEM((panels, order, width), NARROW),
            pltpu.VMEM((panels, nj, order, width), NARROW),
            pltpu.SemaphoreType.DMA((len(rows) + len(cols),)),
        ],
        cost_estimate=cost(
            8 * panels * nj * order * width * width, 2 * panels * (nj + 1) * order * width
        ),
        name="inner_and_mixed",
    )(slots, row_rank, col_rank, low_probe, high_probe, *row_arrays, *col_arrays)


def side_by_side(held, rows, lead=()):
    return jnp.concatenate(
        [held[(k,) + lead + (rows,)] for k in range(held.shape[0])], axis=1
    )


def sketch_body(firsts, slots, mixed_ref, *refs):
    piece_refs, (out_ref, held, sems) = refs[: len(firsts)], refs[len(firsts) :]
    for act in (start, finish):
        each_piece(piece_refs, firsts, slots, 0, held, sems, act)
    mixed = jnp.concatenate([mixed_ref[k] for k in range(mixed_ref.shape[0])], axis=1)
    step = 512
    for at in range(0, held.shape[1], step):
        rows = slice(at, at + step)
        out_ref[:, rows] = rows_by_rows(mixed, side_by_side(held, rows)).astype(NARROW)


def sketch_part(mixed, lefts, order):
    arrays, firsts, slots = unzip(lefts)
    panels, wide, width = mixed.shape
    return pl.pallas_call(
        functools.partial(sketch_body, firsts),
        in_specs=[SMEM, VMEM] + [ANY] * len(arrays),
        out_specs=VMEM,
        out_shape=jax.ShapeDtypeStruct((wide, order), NARROW),
        scratch_shapes=[
            pltpu.VMEM((panels, order, width), NARROW),
            pltpu.SemaphoreType.DMA((len(arrays),)),
        ],
        cost_estimate=cost(2 * panels * wide * order * width, 2 * panels * order * width),
        name="sketch_part",
    )(jnp.stack(slots), mixed, *arrays)


def inverse_factors(grams):
    n, both = grams[0].shape
    lane = lax.broadcasted_iota(jnp.int32, (8, both), 1)
    sub = lax.broadcasted_iota(jnp.int32, (8, both), 0)
    tiles = []
    for m, gram in enumerate(grams):
        one = 0 if m % 2 == 0 else n
        in_one = (lane >= one) & (lane < one + n)
        tiles.append(
            [
                jnp.where(
                    in_one, (lane - one == sub + 8 * t).astype(WIDE), gram[8 * t : 8 * t + 8]
                )
                for t in range(n // 8)
            ]
        )
    for p in range(n):
        t0, q = p // 8, p % 8
        for m, stack in enumerate(tiles):
            at = (n if m % 2 == 0 else 0) + p
            row = stack[t0][q : q + 1]
            row = row / row[:, at : at + 1]
            for t in range(t0, n // 8):
                col = stack[t][:, at : at + 1]
                if t == t0:
                    col = jnp.where(sub[:, :1] > q, col, 0.0)
                stack[t] = stack[t] - col * row
    found = []
    for m, stack in enumerate(tiles):
        one, at = (0, n) if m % 2 == 0 else (n, 0)
        in_one = (lane >= one) & (lane < one + n)
        rows = []
        for t, tile in enumerate(stack):
            pivot = jnp.sum(
                jnp.where(lane - at == sub + 8 * t, tile, 0.0), axis=1, keepdims=True
            )
            rows.append(jnp.where(in_one, tile * lax.rsqrt(pivot), 0.0))
        found.append(jnp.concatenate(rows, axis=0))
    return found


def basis_body(
    firsts, slots, tile_ref, mine_ref, theirs_ref, inner_ref, trail_ref, *refs
):
    np_ = len(firsts)
    piece_refs = refs[:np_]
    basis_out, turned_out, tail_out, left, trail, sampled, basis, sems = refs[np_:]
    order = sampled.shape[1]
    nj = trail.shape[0]
    c = sampled.shape[0] // nj
    panels, _, width = left.shape
    trail_copy = pltpu.make_async_copy(trail_ref, trail, sems.at[np_])
    each_piece(piece_refs, firsts, slots, 0, left, sems, start)
    trail_copy.start()
    exact = lax.Precision.HIGHEST
    sampled[...] = tile_ref[...] - (mine_ref[...].astype(WIDE) + theirs_ref[...].astype(WIDE))
    grams = []
    for j in range(nj):
        mine = sampled[j * c : (j + 1) * c]
        twice = jnp.concatenate([mine, mine], axis=0)
        grams.append(rows_by_rows(mine, twice, exact) * (1.0 / order))
    inverses = inverse_factors(grams)
    for j in range(0, nj, 2):
        pair = jnp.concatenate(inverses[j : j + 2], axis=0)
        rows = slice(j * c, (j + 2) * c)
        basis[rows] = rows_by_columns(pair, sampled[rows], exact).astype(NARROW)
    half = basis_out.shape[1]
    own = pl.multiple_of(slots[np_] * half, half)
    basis_out[...] = basis[:, pl.ds(own, half)]
    each_piece(piece_refs, firsts, slots, 0, left, sems, finish)
    trail_copy.wait()
    for k in range(panels):
        projected = rows_by_columns(basis[...], left[k]).astype(NARROW)
        for j in range(nj):
            turned_out[j * c : (j + 1) * c, k * width : (k + 1) * width] = rows_by_columns(
                projected[j * c : (j + 1) * c], inner_ref[k, :, j * width : (j + 1) * width]
            ).astype(NARROW)
    for j in range(nj):
        both = rows_by_columns(basis[j * c : (j + 1) * c], trail[j])
        moved = pltpu.roll(both, both.shape[1] // 2, 1)
        lane = lax.broadcasted_iota(jnp.int32, moved.shape, 1)
        tail_out[j * c : (j + 1) * c] = jnp.where(
            lane < moved.shape[1] // 2, 0.0, moved
        ).astype(NARROW)


def basis_and_turned(layer, tile, mine, theirs, inner, trail, lefts, half):
    arrays, firsts, slots = unzip(lefts)
    panels, width, _ = inner.shape
    wide, order = mine.shape
    nj, _, both = trail.shape
    return pl.pallas_call(
        functools.partial(basis_body, firsts),
        in_specs=[SMEM, VMEM, VMEM, VMEM, VMEM, ANY] + [ANY] * len(arrays),
        out_specs=[VMEM, VMEM, VMEM],
        out_shape=[
            jax.ShapeDtypeStruct((wide, half), NARROW),
            jax.ShapeDtypeStruct((wide, panels * width), NARROW),
            jax.ShapeDtypeStruct((wide, both), NARROW),
        ],
        scratch_shapes=[
            pltpu.VMEM((panels, order, width), NARROW),
            pltpu.VMEM((nj, order, both), NARROW),
            pltpu.VMEM((wide, order), WIDE),
            pltpu.VMEM((wide, order), NARROW),
            pltpu.SemaphoreType.DMA((len(arrays) + 1,)),
        ],
        cost_estimate=cost(2 * panels * wide * order * width * 8, 2 * panels * order * width),
        name="basis_and_turned",
    )(jnp.stack(slots + [layer]), tile, mine, theirs, inner, trail, *arrays)


def core_body(rows_n, firsts, slots, *refs):
    turned_refs, refs = refs[:rows_n], refs[rows_n:]
    np_ = len(firsts)
    piece_refs = refs[:np_]
    keep_ref, send_ref, left, sems = refs[np_:]
    for act in (start, finish):
        each_piece(piece_refs, firsts, slots, 0, left, sems, act)
    panels, nj, order, width = left.shape
    half = keep_ref.shape[2]
    c = turned_refs[0].shape[0] // nj
    layer = slots[np_]
    for side, out_ref in ((1 - layer, send_ref), (layer, keep_ref)):
        at = pl.multiple_of(side * half, half)
        for j in range(nj):
            turned = jnp.concatenate([t[j * c : (j + 1) * c] for t in turned_refs], axis=0)
            value = rows_by_rows(turned, side_by_side(left, pl.ds(at, half), (j,)))
            for i in range(rows_n):
                out_ref[i, j * c : (j + 1) * c] = value[i * c : (i + 1) * c].astype(NARROW)


def core_parts(layer, turned, lefts, order, half):
    arrays, firsts, slots = unzip(lefts)
    panels, width = sum({f: a.shape[0] for f, a in zip(firsts, arrays)}.values()), arrays[0].shape[-1]
    nj = arrays[0].shape[1]
    wide = turned[0].shape[0]
    shape = jax.ShapeDtypeStruct((len(turned), wide, half), NARROW)
    return pl.pallas_call(
        functools.partial(core_body, len(turned), firsts),
        in_specs=[SMEM] + [VMEM] * len(turned) + [ANY] * len(arrays),
        out_specs=[VMEM, VMEM],
        out_shape=[shape, shape],
        scratch_shapes=[
            pltpu.VMEM((panels, nj, order, width), NARROW),
            pltpu.SemaphoreType.DMA((len(arrays),)),
        ],
        cost_estimate=cost(
            8 * panels * nj * order * width * 128, 2 * panels * nj * order * width
        ),
        name="core_parts",
    )(jnp.stack(slots + [layer]), *turned, *arrays)


def last_body(scale, layer_ref, tail_ref, trail_ref, keep_ref, got_ref, out_ref):
    value = rows_by_rows(tail_ref[0], trail_ref[0, 0])
    value = value - (keep_ref[0].astype(WIDE) + got_ref[0].astype(WIDE))
    out_ref[0] = (value * scale).astype(NARROW)


def last_step(layer, tails, trailing, keep, got):
    ni, nj, order, both = trailing.shape
    c = tails.shape[1] // nj
    half = keep.shape[2]
    flat = pl.BlockSpec((1, c, half), lambda i, j, layer: (i, j, 0))
    return pl.pallas_call(
        functools.partial(last_body, 1.0 / math.sqrt(order)),
        grid_spec=pltpu.PrefetchScalarGridSpec(
            num_scalar_prefetch=1,
            grid=(ni, nj),
            in_specs=[
                pl.BlockSpec((1, c, both), lambda i, j, layer: (i, j, 0)),
                pl.BlockSpec((1, 1, half, both), lambda i, j, layer: (i, j, layer[0], 0)),
                flat,
                flat,
            ],
            out_specs=flat,
        ),
        out_shape=jax.ShapeDtypeStruct((ni, nj * c, half), NARROW),
        cost_estimate=cost(2 * ni * nj * c * half * both, 4 * ni * nj * half * both),
        name="last_step",
    )(layer.reshape(1), tails, trailing, keep, got)


def shards(panel_rows, panel_cols, rank_rows, rank_cols, trailing, sketch):
    panels, ni, _, both = panel_rows.shape
    width = both // 2
    order, c = sketch.shape
    nj = panel_cols.shape[1]
    layers = lax.axis_size("layer")
    layer = lax.axis_index("layer").astype(jnp.int32)
    half = order // layers
    mid = panels // 2
    place = lax.axis_index("row").astype(jnp.int32).reshape(1)
    sketch_t = jnp.swapaxes(sketch, 0, 1)

    col_right, went = square_gather(
        panel_cols[:mid, ..., width:], panel_cols[mid:, ..., width:], "row"
    )
    rights, lefts = [], []
    gate = ()
    for i in range(ni):
        right = line_gather(after(panel_rows[:, i, :, width:], *gate), "col")
        left = line_gather(after(panel_rows[:, i, :, :width], *gate), "col")
        gate = (right[1][0],)
        rights.append(right)
        lefts.append(left)
    gate = went or ()
    col_left, _ = square_gather(
        after(panel_cols[:mid, ..., :width], *gate),
        after(panel_cols[mid:, ..., :width], *gate),
        "row",
    )
    share = probe_share(place, sketch_t, panel_cols)
    low_probe, high_probe = square_sum(share[:mid], share[mid:], "row")
    tiles = tile_samples(sketch_t, trailing)

    bases, turned, tails = [], [], []
    for i in range(ni):
        inner, mixed = inner_and_mixed(
            i, rights[i], col_right, rank_rows, rank_cols, low_probe, high_probe, order
        )
        mine = sketch_part(mixed, lefts[i], order)
        theirs = swap(mine, "layer", 1)
        basis, turn, tail = basis_and_turned(
            layer, tiles[i], mine, theirs, inner, trailing[i], lefts[i], half
        )
        bases.append(basis)
        turned.append(turn)
        tails.append(tail)
    keep, send = core_parts(layer, turned, col_left, order, half)
    got = swap(send, "layer", 1)
    core = last_step(layer, jnp.stack(tails), trailing, keep, got)

    def placed(value):
        return jnp.swapaxes(value.reshape(ni, nj, c, half), 2, 3)

    return placed(jnp.stack(bases)), placed(core)


def solution(mesh):
    specs = (
        P("layer", "row", "col", None),
        P("layer", "col", "row", None),
        P("layer", "row"),
        P("layer", "col"),
        P("row", "col", None, None),
        P(),
    )
    return jax.shard_map(
        shards,
        mesh=mesh,
        in_specs=specs,
        out_specs=(P("row", "col", "layer", None), P("row", "col", "layer", None)),
        check_vma=False,
    )
```

```python
import functools
import math

import jax
import jax.numpy as jnp
from jax import lax
from jax.experimental import pallas as pl
from jax.experimental.pallas import tpu as pltpu
from jax.sharding import PartitionSpec as P


WIDE = jnp.float32
NARROW = jnp.bfloat16
ANY = pl.BlockSpec(memory_space=pl.ANY)
VMEM = pl.BlockSpec(memory_space=pltpu.VMEM)
SMEM = pl.BlockSpec(memory_space=pltpu.SMEM)


def product(a, b, dims, precision=None):
    return lax.dot_general(
        a, b, (dims, ((), ())), precision=precision, preferred_element_type=WIDE
    )


def rows_by_columns(a, b, precision=None):
    return product(a, b, ((1,), (0,)), precision)


def rows_by_rows(a, b, precision=None):
    return product(a, b, ((1,), (1,)), precision)


def cost(flops, moved):
    return pl.CostEstimate(flops=int(flops), bytes_accessed=int(moved), transcendentals=0)


def whole_gather(parts, axis):
    pieces = []
    for first, part in parts:
        full = lax.all_gather(part, axis)
        pieces += [(full[s], first, jnp.int32(s)) for s in range(full.shape[0])]
    return pieces


def swap(part, axis, bit):
    return lax.ppermute(part, axis, [(n, n ^ bit) for n in range(lax.axis_size(axis))])


def line_gather(part, axis):
    if lax.axis_size(axis) != 4:
        return whole_gather([(0, part)], axis)
    place = lax.axis_index(axis)
    outer = (place == 0) | (place == 3)
    ends, middle, outward = [(0, 1), (1, 0), (2, 3), (3, 2)], [(1, 2), (2, 1)], [(1, 0), (2, 3)]
    near = lax.ppermute(part, axis, ends)
    across = lax.ppermute(part, axis, middle)
    across_far = lax.ppermute(near, axis, middle)
    passed = lax.ppermute(across, axis, outward)
    passed_far = lax.ppermute(across_far, axis, outward)
    return [
        (part, 0, place),
        (near, 0, place ^ 1),
        (across, 0, jnp.where(outer, -1, place ^ 3)),
        (across_far, 0, jnp.where(outer, -1, place ^ 2)),
        (passed, 0, jnp.where(outer, place ^ 2, -1)),
        (passed_far, 0, jnp.where(outer, place ^ 3, -1)),
    ]


def square_gather(low, high, axis):
    half = low.shape[0]
    if lax.axis_size(axis) != 4:
        return whole_gather([(0, low), (half, high)], axis)
    place = lax.axis_index(axis)
    low_y, high_x = swap(low, axis, 2), swap(high, axis, 1)
    low_x, high_y = swap(low, axis, 1), swap(high, axis, 2)
    low_far = swap(low_y, axis, 1)
    high_far = swap(high_x, axis, 2)
    return [
        (low, 0, place),
        (high, half, place),
        (low_x, 0, place ^ 1),
        (high_x, half, place ^ 1),
        (low_y, 0, place ^ 2),
        (high_y, half, place ^ 2),
        (low_far, 0, place ^ 3),
        (high_far, half, place ^ 3),
    ]


def square_sum(low, high, axis):
    if lax.axis_size(axis) != 4 or low.shape[1] % 2:
        return lax.psum(low, axis).astype(NARROW), lax.psum(high, axis).astype(NARROW)
    place = lax.axis_index(axis)
    half = low.shape[1] // 2

    def add(part, bit):
        upper = (place & bit) != 0
        begin, end = part[:, :half], part[:, half:]
        mine = jnp.where(upper, end, begin) + swap(jnp.where(upper, begin, end), axis, bit)
        mine = (mine + swap(mine, axis, 3 - bit)).astype(NARROW)
        other = swap(mine, axis, bit)
        return jnp.concatenate(
            [jnp.where(upper, other, mine), jnp.where(upper, mine, other)], axis=1
        )

    return add(low, 1), add(high, 2)


def start_pieces(refs, firsts, slots, base, held, sems, offset=None, by=None, tile=None):
    span = held.shape[-1 if tile is not None else -2]
    for n, (ref, first) in enumerate(zip(refs, firsts)):
        slot = slots[base + n]
        rows = ref.shape[-1 if tile is not None else -2]
        at = slot * rows
        wanted = slot >= 0
        if offset is not None:
            at = at - offset
            wanted = wanted & (at >= 0) & (at < span)

        @pl.when(wanted)
        def _(ref=ref, first=first, at=at, rows=rows):
            lines = (pl.ds(pl.multiple_of(at, rows), rows), slice(None))
            if tile is not None:
                target = held.at[(pl.ds(first, ref.shape[0]), tile) + lines[::-1]]
                pltpu.make_async_copy(ref.at[:, tile], target, sems.at[tile]).start()
            elif by is None:
                lead = (pl.ds(first, ref.shape[0]),) + (slice(None),) * (len(ref.shape) - 3)
                pltpu.make_async_copy(ref, held.at[lead + lines], sems.at[0]).start()
            else:
                for k in range(ref.shape[0]):
                    lead = (first + k,) + (slice(None),) * (len(ref.shape) - 3)
                    pltpu.make_async_copy(ref.at[k], held.at[lead + lines], sems.at[first + k]).start()


def filled(held, sem):
    pltpu.make_async_copy(held, held, sem).wait()


def unzip(pieces):
    arrays, firsts, slots = zip(*pieces)
    return list(arrays), list(firsts), [s.astype(jnp.int32) for s in slots]


def cut_body(plan, *refs):
    count = len(plan)
    panel_refs, out_refs, held, (into, out_of), flipped = (
        refs[:2], refs[2 : 2 + count], refs[2 + count : 2 + 2 * count], refs[2 + 2 * count : 4 + 2 * count],
        list(refs[4 + 2 * count :]),
    )
    moves = []
    for at, (which, first, side, tile, flip) in enumerate(plan):
        width = held[at].shape[-1]
        given = flipped.pop(0) if flip else held[at]
        for n in range(out_refs[at].shape[0]):
            lead = (first + n,) if tile is None else (first + n, tile)
            rows = (slice(None),) * (len(out_refs[at].shape) - 2)
            source = panel_refs[which].at[lead + rows + (pl.ds(side * width, width),)]
            m = len(moves)
            moves.append(
                (
                    pltpu.make_async_copy(source, held[at].at[n], into.at[m]),
                    pltpu.make_async_copy(given.at[n], out_refs[at].at[n], out_of.at[m]),
                    (held[at], given, n) if flip else None,
                )
            )
    for fetch, _, _ in moves:
        fetch.start()
    for fetch, store, flip in moves:
        fetch.wait()
        if flip:
            upright, given, n = flip
            for j in range(given.shape[1]):
                given[n, j] = upright[n, j].T
        store.start()
    for _, store, _ in moves:
        store.wait()


def cut(panel_rows, panel_cols, wanted):
    shapes = []
    for which, _, count, _, tile, _ in wanted:
        _, tiles, rows, both = (panel_rows, panel_cols)[which].shape
        shapes.append((count, tiles, rows, both // 2) if tile is None else (count, rows, both // 2))
    moves = sum(shape[0] for shape in shapes)
    plan = [(which, first, side, tile, flip) for which, first, _, side, tile, flip in wanted]
    flips = [want[-1] for want in wanted]
    given = [shape[:-2] + shape[:-3:-1] if flip else shape for shape, flip in zip(shapes, flips)]
    return pl.pallas_call(
        functools.partial(cut_body, plan),
        in_specs=[ANY, ANY],
        out_specs=[ANY] * len(shapes),
        out_shape=[jax.ShapeDtypeStruct(shape, panel_rows.dtype) for shape in given],
        scratch_shapes=[pltpu.VMEM(shape, panel_rows.dtype) for shape in shapes]
        + [pltpu.SemaphoreType.DMA((moves,)), pltpu.SemaphoreType.DMA((moves,))]
        + [pltpu.VMEM(shape, panel_rows.dtype) for shape, flip in zip(given, flips) if flip],
        cost_estimate=cost(0, 4 * sum(math.prod(shape) for shape in shapes)),
        name="cut",
    )(panel_rows, panel_cols)


def tile_body(sketch_ref, tile_ref, out_ref):
    tile = tile_ref[0, 0]
    both = rows_by_columns(sketch_ref[...], tile)
    turned = pltpu.roll(both, both.shape[1] // 2, 1)
    lane = lax.broadcasted_iota(jnp.int32, turned.shape, 1)
    probe = jnp.where(lane < turned.shape[1] // 2, turned, 0.0).astype(NARROW)
    out_ref[0] = rows_by_rows(probe, tile)


def tile_samples(sketch_t, trailing):
    ni, nj, order, both = trailing.shape
    c = sketch_t.shape[0]
    return pl.pallas_call(
        tile_body,
        grid=(ni, nj),
        in_specs=[
            pl.BlockSpec((c, order), lambda i, j: (0, 0)),
            pl.BlockSpec((1, 1, order, both), lambda i, j: (i, j, 0, 0)),
        ],
        out_specs=pl.BlockSpec((1, c, order), lambda i, j: (i, j, 0)),
        out_shape=jax.ShapeDtypeStruct((ni, nj * c, order), WIDE),
        cost_estimate=cost(4 * ni * nj * order * both * c, 4 * ni * nj * order * both),
        name="tile_samples",
    )(sketch_t, trailing)


def probe_body(place_ref, sketch_ref, left_ref, out_ref):
    for j in range(left_ref.shape[1]):
        out_ref[0, j] = rows_by_columns(sketch_ref[...], left_ref[0, j])


def probe_share(place, sketch_t, panel):
    k, nj, rows, both = panel.shape
    c = sketch_t.shape[0]
    width = both // 2
    return pl.pallas_call(
        probe_body,
        grid_spec=pltpu.PrefetchScalarGridSpec(
            num_scalar_prefetch=1,
            grid=(k,),
            in_specs=[
                pl.BlockSpec((c, rows), lambda n, place: (0, place[0])),
                pl.BlockSpec((1, nj, rows, width), lambda n, place: (n, 0, 0, 0)),
            ],
            out_specs=pl.BlockSpec((1, nj, c, width), lambda n, place: (n, 0, 0, 0)),
        ),
        out_shape=jax.ShapeDtypeStruct((k, nj, c, width), WIDE),
        cost_estimate=cost(2 * k * nj * rows * width * c, 2 * k * nj * rows * width),
        name="probe_share",
    )(place, sketch_t, panel)


def inner_body(
    row, row_firsts, col_firsts, slots, row_rank, col_rank, low_probe, high_probe, *refs
):
    nr, nc = len(row_firsts), len(col_firsts)
    row_refs, col_refs = refs[:nr], refs[nr : nr + nc]
    inner_ref, mixed_ref, row_held, col_held, row_sems, col_sems = refs[nr + nc :]
    start_pieces(row_refs, row_firsts, slots, 0, row_held, row_sems, by=0)
    start_pieces(col_refs, col_firsts, slots, nr, col_held, col_sems, by=0)
    panels, nj = col_held.shape[:2]
    width = col_held.shape[-1]
    half = low_probe.shape[0]

    def one(k, probe_ref, n):
        filled(row_held.at[k], row_sems.at[k])
        filled(col_held.at[k], col_sems.at[k])
        right = jnp.concatenate([col_held[k, j] for j in range(nj)], axis=1)
        value = product(row_held[k], right, ((0,), (0,)))
        r = lax.broadcasted_iota(jnp.int32, (width, width), 0)
        s = lax.broadcasted_iota(jnp.int32, (width, width), 1)
        mixed = []
        for j in range(nj):
            kept = (r < row_rank[k, row]) & (s < col_rank[k, j])
            block = jnp.where(kept, value[:, j * width : (j + 1) * width], 0.0).astype(NARROW)
            inner_ref[k, :, j * width : (j + 1) * width] = block
            mixed.append(rows_by_rows(probe_ref[n, j], block))
        mixed_ref[k] = jnp.concatenate(mixed, axis=0).astype(NARROW)

    @pl.loop(0, half)
    def _(n):
        one(n, low_probe, n)

    @pl.loop(0, panels - half)
    def _(n):
        one(n + half, high_probe, n)


def inner_and_mixed(row, rows, cols, row_rank, col_rank, low_probe, high_probe, order):
    row_arrays, row_firsts, row_slots = unzip(rows)
    col_arrays, col_firsts, col_slots = unzip(cols)
    slots = jnp.stack(row_slots + col_slots)
    panels, width = row_arrays[0].shape[0], row_arrays[0].shape[-1]
    nj = col_arrays[0].shape[1]
    c = low_probe.shape[2]
    return pl.pallas_call(
        functools.partial(inner_body, row, row_firsts, col_firsts),
        in_specs=[SMEM, SMEM, SMEM, VMEM, VMEM] + [ANY] * (len(rows) + len(cols)),
        out_specs=[VMEM, VMEM],
        out_shape=[
            jax.ShapeDtypeStruct((panels, width, nj * width), NARROW),
            jax.ShapeDtypeStruct((panels, nj * c, width), NARROW),
        ],
        scratch_shapes=[
            pltpu.VMEM((panels, order, width), NARROW),
            pltpu.VMEM((panels, nj, order, width), NARROW),
            pltpu.SemaphoreType.DMA((panels,)),
            pltpu.SemaphoreType.DMA((panels,)),
        ],
        cost_estimate=cost(
            8 * panels * nj * order * width * width, 2 * panels * (nj + 1) * order * width
        ),
        name="inner_and_mixed",
    )(slots, row_rank, col_rank, low_probe, high_probe, *row_arrays, *col_arrays)


def side_by_side(held, rows, lead=()):
    return jnp.concatenate(
        [held[(k,) + lead + (rows,)] for k in range(held.shape[0])], axis=1
    )


def sketch_body(slots, mixed_ref, *refs):
    count = len(refs) - 7
    piece_refs, (out_ref, mixed_held, held, value, sems, stores, mixed_sem) = refs[:count], refs[count:]
    mixed_copy = pltpu.make_async_copy(mixed_ref, mixed_held, mixed_sem)
    mixed_copy.start()
    rows = piece_refs[0].shape[1]

    def fetch(n):
        return pltpu.make_async_copy(piece_refs[n], held.at[n], sems.at[n])

    def store(n):
        lanes = pl.ds(pl.multiple_of(slots[n] * rows if count > 1 else 0, rows), rows)
        return pltpu.make_async_copy(value.at[n], out_ref.at[:, lanes], stores.at[n])

    for n in range(count):

        @pl.when(slots[n] >= 0)
        def _(n=n):
            fetch(n).start()

    mixed_copy.wait()
    mixed = jnp.concatenate([mixed_held[k] for k in range(mixed_held.shape[0])], axis=1)
    for n in range(count):

        @pl.when(slots[n] >= 0)
        def _(n=n):
            fetch(n).wait()
            value[n] = rows_by_rows(mixed, side_by_side(held.at[n], slice(None))).astype(NARROW)
            store(n).start()

    for n in range(count):

        @pl.when(slots[n] >= 0)
        def _(n=n):
            store(n).wait()


def sketch_part(mixed, lefts, order):
    arrays, _, slots = unzip(lefts)
    count = len(arrays)
    panels, wide, width = mixed.shape
    rows = arrays[0].shape[1]
    return pl.pallas_call(
        sketch_body,
        in_specs=[SMEM, ANY] + [ANY] * count,
        out_specs=ANY,
        out_shape=jax.ShapeDtypeStruct((wide, order if count > 1 else rows), NARROW),
        scratch_shapes=[
            pltpu.VMEM(mixed.shape, NARROW),
            pltpu.VMEM((count, panels, rows, width), NARROW),
            pltpu.VMEM((count, wide, rows), NARROW),
            pltpu.SemaphoreType.DMA((count,)),
            pltpu.SemaphoreType.DMA((count,)),
            pltpu.SemaphoreType.DMA(()),
        ],
        cost_estimate=cost(2 * panels * wide * order * width, 2 * panels * order * width),
        name="sketch_part",
    )(jnp.stack(slots), mixed, *arrays)


def inverse_factors(grams):
    n, both = grams[0].shape
    lane = lax.broadcasted_iota(jnp.int32, (8, both), 1)
    sub = lax.broadcasted_iota(jnp.int32, (8, both), 0)
    tiles = []
    for m, gram in enumerate(grams):
        one = 0 if m % 2 == 0 else n
        in_one = (lane >= one) & (lane < one + n)
        tiles.append(
            [
                jnp.where(
                    in_one, (lane - one == sub + 8 * t).astype(WIDE), gram[8 * t : 8 * t + 8]
                )
                for t in range(n // 8)
            ]
        )
    for p in range(0, n, 2):
        t0, q = p // 8, p % 8
        for m, stack in enumerate(tiles):
            at = (n if m % 2 == 0 else 0) + p
            upper, lower = stack[t0][q : q + 1], stack[t0][q + 1 : q + 2]
            a, b, d = upper[:, at : at + 1], lower[:, at : at + 1], lower[:, at + 1 : at + 2]
            scale = 1.0 / (a * d - b * b)
            first = (d * upper - b * lower) * scale
            second = (a * lower - b * upper) * scale
            for t in range(t0, n // 8):
                tile = stack[t]
                change = tile[:, at : at + 1] * first + tile[:, at + 1 : at + 2] * second
                if t == t0:
                    change = jnp.where(sub > q + 1, change, 0.0)
                stack[t] = tile - change
    found = []
    for m, stack in enumerate(tiles):
        one, at = (0, n) if m % 2 == 0 else (n, 0)
        in_one = (lane >= one) & (lane < one + n)
        odd = sub[:, :1] % 2 == 1
        rows = []
        for t, tile in enumerate(stack):
            row = sub + 8 * t

            def at_lane(value, shift):
                return jnp.sum(jnp.where(lane - at == row - shift, value, 0.0), axis=1, keepdims=True)

            pivot, beside = at_lane(tile, 0), at_lane(tile, 1)
            above = pltpu.roll(tile, 1, 0)
            ratio = jnp.where(odd, beside / at_lane(above, 1), 0.0)
            tile = tile - ratio * above
            pivot = pivot - ratio * beside
            rows.append(jnp.where(in_one, tile * lax.rsqrt(pivot), 0.0))
        found.append(jnp.concatenate(rows, axis=0))
    return found


def split(value):
    high = value.astype(NARROW)
    return high, (value - high.astype(WIDE)).astype(NARROW)


def find_basis(c, tile, mine, theirs, parts, basis, late=None):
    wide, order = tile.shape
    pair = 2 * c
    inverses = []
    for p in range(wide // pair):
        rows = slice(p * pair, (p + 1) * pair)
        high, low = split(tile[rows] - (mine[rows].astype(WIDE) + theirs[rows].astype(WIDE)))
        parts[p, :pair] = high
        parts[p, pair:] = low
    if late:
        slot, mine_late, theirs_late = late
        span = mine_late.shape[1]

        @pl.when(slot >= 0)
        def _():
            lanes = pl.ds(pl.multiple_of(slot * span, span), span)
            for p in range(wide // pair):
                rows = slice(p * pair, (p + 1) * pair)
                group = mine_late[rows].astype(WIDE) + theirs_late[rows].astype(WIDE)
                high, low = split(tile[rows, lanes] - group)
                parts[p, :pair, lanes] = high
                parts[p, pair:, lanes] = low

    for p in range(wide // pair):
        products = rows_by_rows(parts[p, :pair], parts[p])
        cross = products[:, pair:]
        gram = (products[:, :pair] + (cross + cross.T)) * (1.0 / order)
        gram = pltpu.roll(gram, c, 1)
        inverses += [gram[:c], gram[c:]]
    inverses = inverse_factors(inverses)
    step = 512
    for p in range(wide // pair):
        high, low = split(jnp.concatenate(inverses[2 * p : 2 * p + 2], axis=0))
        factor = jnp.concatenate(
            [
                jnp.concatenate([high, high], axis=1),
                jnp.concatenate([low, jnp.zeros_like(low)], axis=1),
            ],
            axis=0,
        )
        for at in range(0, order, step):
            value = rows_by_columns(factor, parts[p, :, at : at + step])
            basis[p * pair : (p + 1) * pair, at : at + step] = (value[:pair] + value[pair:]).astype(NARROW)


def turn(c, basis, inner, left, trail, turned, tail):
    panels, _, width = left.shape
    nj = trail.shape[0]
    for k in range(0, panels, 2):
        both = jnp.concatenate([left[n] for n in range(k, min(k + 2, panels))], axis=1)
        projected = rows_by_columns(basis[...], both).astype(NARROW)
        for n in range(both.shape[1] // width):
            for j in range(nj):
                turned[j * c : (j + 1) * c, (k + n) * width : (k + n + 1) * width] = rows_by_columns(
                    projected[j * c : (j + 1) * c, n * width : (n + 1) * width],
                    inner[k + n, :, j * width : (j + 1) * width],
                ).astype(NARROW)
    for j in range(nj):
        both = rows_by_columns(basis[j * c : (j + 1) * c], trail[j])
        moved = pltpu.roll(both, both.shape[1] // 2, 1)
        lane = lax.broadcasted_iota(jnp.int32, moved.shape, 1)
        tail[j * c : (j + 1) * c] = jnp.where(
            lane < moved.shape[1] // 2, 0.0, moved
        ).astype(NARROW)


def basis_body(row, firsts, layers, apart, slots, *refs):
    np_ = len(firsts)
    tile_ref, mine_ref, theirs_ref, inner_ref, trail_ref = refs[:5]
    refs = refs[6 if row else 5 :]
    late = None
    if apart:
        mine_late, theirs_late = refs[:2]
        refs, (mine_held, theirs_held) = refs[2:-2], refs[-2:]
        late = (slots[np_ - 1], mine_held, theirs_held)
    piece_refs = refs[:np_]
    basis_out, turned, tail, tile, mine, theirs, inner, left, trail, parts, basis, own, sems, local = refs[np_:]
    half = tile.shape[1] // layers
    c = tile.shape[0] // trail.shape[0]
    start_at = pl.multiple_of(slots[np_] * half, half)
    copies = [
        pltpu.make_async_copy(tile_ref.at[row], tile, local.at[0]),
        pltpu.make_async_copy(mine_ref, mine, local.at[1]),
        pltpu.make_async_copy(theirs_ref, theirs, local.at[2]),
        pltpu.make_async_copy(inner_ref, inner, local.at[3]),
        pltpu.make_async_copy(trail_ref.at[row], trail, local.at[4]),
    ]
    first = copies[:3]
    if apart:
        first += [
            pltpu.make_async_copy(mine_late, mine_held, local.at[6]),
            pltpu.make_async_copy(theirs_late, theirs_held, local.at[7]),
        ]
    for copy in first:
        copy.start()
    for copy in first:
        copy.wait()
    for copy in copies[3:]:
        copy.start()
    start_pieces(piece_refs, firsts, slots, 0, left, sems)
    find_basis(c, tile, mine, theirs, parts, basis, late)
    own[...] = basis[:, pl.ds(start_at, half)]
    keep = pltpu.make_async_copy(own, basis_out.at[row], local.at[5])
    keep.start()
    for copy in copies[3:]:
        copy.wait()
    filled(left, sems.at[0])
    turn(c, basis, inner, left, trail, turned, tail)
    keep.wait()


def basis_and_turned(layers, layer, row, tiles, mine, theirs, inner, trailing, lefts, bases, late=()):
    arrays, firsts, slots = unzip(lefts)
    panels, width, _ = inner.shape
    wide, order = mine.shape
    ni, nj, _, both = trailing.shape
    half = order // layers
    return pl.pallas_call(
        functools.partial(basis_body, row, firsts, layers, bool(late)),
        in_specs=[SMEM] + [ANY] * (5 + (1 if row else 0) + len(late) + len(arrays)),
        out_specs=[ANY, VMEM, VMEM],
        out_shape=[
            jax.ShapeDtypeStruct((ni, wide, half), NARROW),
            jax.ShapeDtypeStruct((wide, panels * width), NARROW),
            jax.ShapeDtypeStruct((wide, both), NARROW),
        ],
        scratch_shapes=[
            pltpu.VMEM((wide, order), WIDE),
            pltpu.VMEM((wide, order), NARROW),
            pltpu.VMEM((wide, order), NARROW),
            pltpu.VMEM(inner.shape, NARROW),
            pltpu.VMEM((panels, order, width), NARROW),
            pltpu.VMEM((nj, order, both), NARROW),
            pltpu.VMEM((nj // 2, 4 * (wide // nj), order), NARROW),
            pltpu.VMEM((wide, order), NARROW),
            pltpu.VMEM((wide, half), NARROW),
            pltpu.SemaphoreType.DMA((1,)),
            pltpu.SemaphoreType.DMA((8,)),
        ]
        + [pltpu.VMEM(part.shape, NARROW) for part in late],
        input_output_aliases={6: 0} if row else {},
        cost_estimate=cost(2 * panels * wide * order * width * 8, 2 * panels * order * width),
        name="basis_and_turned",
    )(
        jnp.stack(slots + [layer]), tiles, mine, theirs, inner, trailing,
        *([bases] if row else []), *late, *arrays,
    )


def core_body(rows_n, firsts, with_tile, slots, *refs):
    refs = list(refs)

    def take(n):
        got = refs[:n]
        del refs[:n]
        return got

    turned_refs = take(rows_n)
    if with_tile:
        (trail_ref,), tail_refs = take(1), take(rows_n)
    piece_refs = take(len(firsts))
    out_ref, left, held, turned, sems, stores, small = take(7)
    nj, half = left.shape[1], left.shape[3]
    c = out_ref.shape[1] // nj
    offset = slots[len(firsts)] * half
    copies = [
        pltpu.make_async_copy(ref, turned.at[i], small.at[i]) for i, ref in enumerate(turned_refs)
    ]
    if with_tile:
        trail, tails = take(2)
        rows = pl.ds(pl.multiple_of(offset, half), half)
        copies += [
            pltpu.make_async_copy(ref, tails.at[i], small.at[rows_n + i])
            for i, ref in enumerate(tail_refs)
        ]
        copies.append(
            pltpu.make_async_copy(trail_ref.at[:, :, rows, :], trail, small.at[2 * rows_n])
        )
    for copy in copies[:rows_n]:
        copy.start()
    for j in range(nj):
        start_pieces(piece_refs, firsts, slots, 0, left, sems, offset, tile=j)
        if j == 0:
            for copy in copies[rows_n:]:
                copy.start()
    for copy in copies[:rows_n]:
        copy.wait()
    moves = []
    for j in range(nj):
        group = slice(j * c, (j + 1) * c)
        both = jnp.concatenate([turned[i, group] for i in range(rows_n)], axis=0)
        filled(left.at[:, j], sems.at[j])
        stacked = jnp.concatenate([left[k, j] for k in range(left.shape[0])], axis=0)
        value = rows_by_columns(both, stacked).astype(NARROW)
        if j == 0:
            for copy in copies[rows_n:]:
                copy.wait()
        for i in range(rows_n):
            mine = value[i * c : (i + 1) * c]
            if with_tile:
                mine = rows_by_rows(tails[i, group], trail[i, j]) - mine.astype(WIDE)
            held[i, group] = mine
        moves.append(pltpu.make_async_copy(held.at[:, group], out_ref.at[:, group], stores.at[j]))
        moves[-1].start()
    for move in moves:
        move.wait()


def core_half(side, turned, lefts, half, tails=(), trailing=None):
    arrays, firsts, slots = unzip(lefts)
    panels = sum({f: a.shape[0] for f, a in zip(firsts, arrays)}.values())
    nj, width = arrays[0].shape[1:3]
    ni, wide = len(turned), turned[0].shape[0]
    with_tile = trailing is not None
    kind = WIDE if with_tile else NARROW
    scratch = [
        pltpu.VMEM((panels, nj, width, half), NARROW),
        pltpu.VMEM((ni, wide, half), kind),
        pltpu.VMEM((ni,) + turned[0].shape, NARROW),
        pltpu.SemaphoreType.DMA((nj,)),
        pltpu.SemaphoreType.DMA((nj,)),
        pltpu.SemaphoreType.DMA((2 * ni + 1,)),
    ]
    if with_tile:
        scratch += [
            pltpu.VMEM((ni, nj, half, trailing.shape[-1]), NARROW),
            pltpu.VMEM((ni,) + tails[0].shape, NARROW),
        ]
    return pl.pallas_call(
        functools.partial(core_body, ni, firsts, with_tile),
        in_specs=[SMEM] + [ANY] * (ni + (1 + ni if with_tile else 0) + len(arrays)),
        out_specs=ANY,
        out_shape=jax.ShapeDtypeStruct((ni, wide, half), kind),
        scratch_shapes=scratch,
        cost_estimate=cost(
            4 * panels * nj * half * width * 128, 2 * panels * nj * half * width
        ),
        name="core_half",
    )(
        jnp.stack(slots + [side]), *turned,
        *([trailing, *tails] if with_tile else []), *arrays,
    )


def shards(panel_rows, panel_cols, rank_rows, rank_cols, trailing, sketch):
    panels, ni, _, _ = panel_rows.shape
    order, c = sketch.shape
    nj = panel_cols.shape[1]
    layers = lax.axis_size("layer")
    layer = lax.axis_index("layer").astype(jnp.int32)
    half = order // layers
    mid = panels // 2
    place = lax.axis_index("row").astype(jnp.int32).reshape(1)
    sketch_t = jnp.swapaxes(sketch, 0, 1)

    def low_high(side, flip):
        return [(1, 0, mid, side, None, flip), (1, mid, panels - mid, side, None, flip)]

    def row_tile(i, side):
        return (0, 0, panels, side, i, False)

    (first,) = cut(panel_rows, panel_cols, [row_tile(0, 1)])
    low, high = cut(panel_rows, panel_cols, low_high(1, False))
    (first_left,) = cut(panel_rows, panel_cols, [row_tile(0, 0)])
    rights = [line_gather(first, "col")]
    lefts = [line_gather(first_left, "col")]
    col_right = square_gather(low, high, "row")
    wanted = [row_tile(i, side) for i in range(1, ni) for side in (1, 0)] + low_high(0, True)
    *parts, low, high = cut(panel_rows, panel_cols, wanted)
    for i in range(1, ni):
        rights.append(line_gather(parts[2 * i - 2], "col"))
        lefts.append(line_gather(parts[2 * i - 1], "col"))
    col_left = square_gather(low, high, "row")
    share = probe_share(place, sketch_t, panel_cols)
    low_probe, high_probe = square_sum(share[:mid], share[mid:], "row")
    tiles = tile_samples(sketch_t, trailing)

    bases, turned, tails = None, [], []
    for i in range(ni):
        inner, mixed = inner_and_mixed(
            i, rights[i], col_right, rank_rows, rank_cols, low_probe, high_probe, order
        )
        early = lefts[i][: -1 if i == ni - 1 else None]
        mine = sketch_part(mixed, early, order)
        theirs = swap(mine, "layer", 1)
        late = ()
        if i == ni - 1:
            mine_late = sketch_part(mixed, lefts[i][-1:], order)
            late = (mine_late, swap(mine_late, "layer", 1))
        bases, turn_, tail = basis_and_turned(
            layers, layer, i, tiles, mine, theirs, inner, trailing, lefts[i], bases, late
        )
        turned.append(turn_)
        tails.append(tail)
    give = core_half(1 - layer, turned, col_left, half)
    got = swap(give, "layer", 1)
    own = core_half(layer, turned, col_left, half, tails, trailing)
    core = ((own - got.astype(WIDE)) * (1.0 / math.sqrt(order))).astype(NARROW)

    def placed(value):
        return jnp.swapaxes(value.reshape(ni, nj, c, half), 2, 3)

    return placed(bases), placed(core)


def solution(mesh):
    specs = (
        P("layer", "row", "col", None),
        P("layer", "col", "row", None),
        P("layer", "row"),
        P("layer", "col"),
        P("row", "col", None, None),
        P(),
    )
    return jax.shard_map(
        shards,
        mesh=mesh,
        in_specs=specs,
        out_specs=(P("row", "col", "layer", None), P("row", "col", "layer", None)),
        check_vma=False,
    )
```
